32 devices in a mesh: dp: 8 (over z, x), seq: 4 (over y, core).
Axes of the slice: x: 2, y: 2, z: 4, core: 2. Of those that a mesh axis runs over, the one named last changes fastest.
Arguments:
- hidden: bfloat16 [16, 640, 1536], P('dp', 'seq'), may hold values from -6 to 6
- conditioning: bfloat16 [15, 130, 768], replicated, may hold values from -6 to 6
- slot_sequence: int32 [16], P('dp'), may hold values from 0 to 15, each once
- lengths: int32 [15], replicated, may hold values from 318 to 637, as said below
- self_inputs: bfloat16 [1536, 4608], P('dp'), may hold values from -0.15625 to 0.15625
- self_output: bfloat16 [1536, 1536], P('dp'), may hold values from -0.625 to 0.625
- cross_query: bfloat16 [1536, 1536], P('dp'), may hold values from -0.15625 to 0.15625
- cross_memory: bfloat16 [768, 3072], P('dp'), may hold values from -0.21875 to 0.21875
- cross_output: bfloat16 [1536, 1536], P('dp'), may hold values from -0.4375 to 0.4375
- feed_expand: bfloat16 [1536, 12288], P('dp'), may hold values from -0.15625 to 0.15625
- feed_reduce: bfloat16 [6144, 1536], P('dp'), may hold values from -0.078125 to 0.078125
- gain_self: bfloat16 [1536], P('dp'), may hold values from 0.5 to 1.5
- gain_cross: bfloat16 [1536], P('dp'), may hold values from 0.5 to 1.5
- gain_feed: bfloat16 [1536], P('dp'), may hold values from 0.5 to 1.5
- cotangent: bfloat16 [16, 640, 1536], P('dp', 'seq'), may hold values from -6 to 6
Outputs:
- output: bfloat16 [16, 640, 1536], P('dp', 'seq')
- grad_hidden: float32 [16, 640, 1536], P('dp', 'seq')
- grad_self_inputs: float32 [1536, 4608], P('dp')
- grad_self_output: float32 [1536, 1536], P('dp')
- grad_cross_query: float32 [1536, 1536], P('dp')
- grad_cross_memory: float32 [768, 3072], P('dp')
- grad_cross_output: float32 [1536, 1536], P('dp')
- grad_feed_expand: float32 [1536, 12288], P('dp')
- grad_feed_reduce: float32 [6144, 1536], P('dp')
- grad_gain_self: float32 [1536], P('dp')
- grad_gain_cross: float32 [1536], P('dp')
- grad_gain_feed: float32 [1536], P('dp')
The draws below stay inside these ranges and needn't reach their ends.
Inputs may be any that keep to these rules, and one draw needn't show every extreme that they name: Slot s holds sequence slot_sequence[s]; each value appears once, and the value 15 marks the one empty slot. `lengths`: one sequence in every draw has exactly 637 valid tokens.
All inputs are finite; a program needn't handle non-finite values.
Results may differ from the reference program's by a relative error of at most 0.025.
Values may be sent and summed in bfloat16 or wider, within the bound.
No kernel may reach another device: no remote copies, remote signals or barrier semaphores. Data moves between devices by JAX's collectives and lax.ppermute only.
A program may use at most 304 MiB of HBM per device.

```python
import math
import jax
import jax.numpy as jnp
from jax import lax

D = 1536
H = 24
HD = 64
FF = 6144
DC = 768
CT = 130
LEN = 640
SEQ_LEN = 637
SLOTS = 16
SEQS = 15


def draw_lengths(key, part):
    drawn = jax.random.randint(key, (SEQS,), SEQ_LEN // 2, SEQ_LEN + 1, dtype=jnp.int32)
    chosen = jax.random.randint(jax.random.fold_in(key, 7), (), 0, SEQS, dtype=jnp.int32)
    return jnp.where(jnp.arange(SEQS, dtype=jnp.int32) == chosen, jnp.int32(SEQ_LEN), drawn)


def levels(own_key, extent, pieces, least, top_value):
    level, own = 1.0, jax.random.fold_in(own_key, 6)
    for position, shards_of in pieces:
        heights = jnp.exp(jax.random.uniform(jax.random.fold_in(own, position), (shards_of,), jnp.float32, least / len(pieces), top_value / len(pieces)))
        level = level * jnp.repeat(heights, extent[position] // shards_of).reshape([-1 if axis == position else 1 for axis in range(len(extent))])
    return level


def bell_draw(rng, dims, spread, most, cuts=(), held_as=jnp.bfloat16):
    level = levels(rng, dims, cuts, -0.22, 0.18) if cuts else 1.0
    entries = jax.random.normal(rng, dims, jnp.float32) * spread * level
    return jnp.minimum(jnp.maximum(entries, -most), most).astype(held_as)


def setup_inputs(seed: int = 0) -> dict:
    keys = jax.random.split(jax.random.key(seed), 16)
    return {
        "hidden": bell_draw(keys[0], (SLOTS, LEN, D), 1.0, 6.0, ((0, 8), (1, 4))),
        "conditioning": bell_draw(keys[1], (SEQS, CT, DC), 1.0, 6.0),
        "slot_sequence": jax.random.permutation(keys[2], SLOTS).astype(jnp.int32),
        "lengths": draw_lengths(jax.random.fold_in(keys[15], 71), 0),
        "self_inputs": bell_draw(keys[4], (D, 3 * D), D ** -0.5, 0.15625, ((0, 8),)),
        "self_output": bell_draw(keys[5], (D, D), (D // 16) ** -0.5, 0.625, ((0, 8),)),
        "cross_query": bell_draw(keys[6], (D, D), D ** -0.5, 0.15625, ((0, 8),)),
        "cross_memory": bell_draw(keys[7], (DC, 2 * D), DC ** -0.5, 0.21875, ((0, 8),)),
        "cross_output": bell_draw(keys[8], (D, D), (D // 8) ** -0.5, 0.4375, ((0, 8),)),
        "feed_expand": bell_draw(keys[9], (D, 2 * FF), D ** -0.5, 0.15625, ((0, 8),)),
        "feed_reduce": bell_draw(keys[10], (FF, D), FF ** -0.5, 0.078125, ((0, 8),)),
        "gain_self": jnp.clip(1.0 + 0.1 * jax.random.normal(keys[11], (D,), jnp.float32), 0.5, 1.5).astype(jnp.bfloat16),
        "gain_cross": jnp.clip(1.0 + 0.1 * jax.random.normal(keys[12], (D,), jnp.float32), 0.5, 1.5).astype(jnp.bfloat16),
        "gain_feed": jnp.clip(1.0 + 0.1 * jax.random.normal(keys[13], (D,), jnp.float32), 0.5, 1.5).astype(jnp.bfloat16),
        "cotangent": bell_draw(keys[14], (SLOTS, LEN, D), 1.0, 6.0, ((0, 8), (1, 4))),
    }


@jax.custom_vjp
def low(v):
    return lax.optimization_barrier(v.astype(jnp.bfloat16)).astype(jnp.float32)

@jax.custom_vjp
def low_back(v):
    return v

def low_keep(v):
    return (low(v), None)

def low_pass(kept, grad):
    return (grad,)

def back_keep(v):
    return (v, None)

def back_low(kept, grad):
    return (low(grad),)
low.defvjp(low_keep, low_pass)
low_back.defvjp(back_keep, back_low)
EPSILON = 1e-05
NEGATIVE = -1e+30
HIGHEST = lax.Precision.HIGHEST

def product(operand_a, operand_b):
    return jnp.dot(operand_a, operand_b, precision=HIGHEST, preferred_element_type=jnp.float32)

def layer_norm(values, gain):
    centred = values - lax.optimization_barrier(jnp.mean(values, axis=-1, keepdims=True))
    return centred * lax.rsqrt(lax.optimization_barrier(jnp.mean(centred * centred, axis=-1, keepdims=True)) + EPSILON) * gain

def rotary(count):
    freqs = jnp.exp(jnp.arange(HD // 2, dtype=jnp.float32) * (-2.0 * math.log(10000.0) / HD))
    angles = jnp.arange(count, dtype=jnp.float32)[:, None] * freqs[None, :]
    return (jnp.cos(angles)[:, None, :], jnp.sin(angles)[:, None, :])

def rotate(values, cosine, sine):
    half = values.shape[-1] // 2
    first = values[..., :half]
    second = values[..., half:]
    return jnp.concatenate([first * cosine - second * sine, first * sine + second * cosine], axis=-1)

def softmax_rows(scores):
    shifted = jnp.exp(scores - lax.optimization_barrier(jnp.max(scores, axis=-1, keepdims=True)))
    return shifted / lax.optimization_barrier(jnp.sum(shifted, axis=-1, keepdims=True))

def slot_forward(weights, hidden_rows, memory, length):
    self_inputs, self_output, cross_query, cross_memory, cross_output, feed_expand, feed_reduce, gain_self, gain_cross, gain_feed = weights
    count = hidden_rows.shape[0]
    cosine, sine = rotary(count)
    positions = jnp.arange(count, dtype=jnp.int32)
    usable = (positions < jnp.maximum(length, 1))[None, None, :]
    valid = (positions < length).astype(jnp.float32)[:, None]
    scale = HD ** (-0.5)
    normed_one = low(layer_norm(hidden_rows, gain_self))
    triple = low(low_back(product(normed_one, self_inputs))).reshape(count, 3, H, HD)
    queries = low(rotate(triple[:, 0], cosine, sine))
    keys_rot = low(rotate(triple[:, 1], cosine, sine))
    scores = low_back(jnp.einsum('qhd,khd->hqk', queries, keys_rot, precision=HIGHEST) * scale)
    probs = low(softmax_rows(jnp.where(usable, scores, NEGATIVE)))
    attended = jnp.einsum('hqk,khd->qhd', probs, triple[:, 2], precision=HIGHEST)
    context = low(low_back(attended.reshape(count, D)))
    after_self = hidden_rows + low_back(product(context, self_output))
    normed_two = low(layer_norm(after_self, gain_cross))
    cross_q = low(low_back(product(normed_two, cross_query))).reshape(count, H, HD)
    memory_kv = low(product(memory, cross_memory))
    memory_keys = memory_kv[:, :D].reshape(CT, H, HD)
    memory_vals = memory_kv[:, D:].reshape(CT, H, HD)
    cross_scores = low_back(jnp.einsum('qhd,khd->hqk', cross_q, memory_keys, precision=HIGHEST) * scale)
    cross_probs = low(softmax_rows(cross_scores))
    cross_att = jnp.einsum('hqk,khd->qhd', cross_probs, memory_vals, precision=HIGHEST)
    cross_ctx = low(low_back(cross_att.reshape(count, D)))
    after_cross = after_self + low_back(product(cross_ctx, cross_output))
    normed_three = low(layer_norm(after_cross, gain_feed))
    expanded = low_back(product(normed_three, feed_expand))
    gate_part = expanded[:, :FF]
    up_part = expanded[:, FF:]
    activated = low(gate_part / (1.0 + jnp.exp(-gate_part)) * up_part)
    result = after_cross + low_back(product(activated, feed_reduce))
    return result * valid

def reference(hidden, conditioning, slot_sequence, lengths, self_inputs, self_output, cross_query, cross_memory, cross_output, feed_expand, feed_reduce, gain_self, gain_cross, gain_feed, cotangent):
    weights = tuple((item.astype(jnp.float32) for item in (self_inputs, self_output, cross_query, cross_memory, cross_output, feed_expand, feed_reduce, gain_self, gain_cross, gain_feed)))
    table = jnp.arange(SEQS, dtype=jnp.int32)

    def one_slot(totals, items):
        hidden_rows, cotangent_rows, sequence = items
        length = jnp.sum(jnp.where(table == sequence, lengths, 0)).astype(jnp.int32)
        index = jnp.minimum(sequence, SEQS - 1).astype(jnp.int32)
        memory = lax.dynamic_index_in_dim(conditioning, index, 0, keepdims=False).astype(jnp.float32)

        def forward(weight_set, rows_in):
            return slot_forward(weight_set, rows_in, memory, length)
        output_rows, pull = jax.vjp(forward, weights, hidden_rows.astype(jnp.float32))
        grad_weights, grad_rows = pull(cotangent_rows.astype(jnp.float32))
        totals = jax.tree.map(jnp.add, totals, grad_weights)
        return (totals, (output_rows.astype(jnp.bfloat16), grad_rows))
    start = tuple((jnp.zeros(item.shape, jnp.float32) for item in weights))
    totals, stacked = lax.scan(one_slot, start, (hidden, cotangent, slot_sequence))
    return (stacked[0], stacked[1], totals[0], totals[1], totals[2], totals[3], totals[4], totals[5], totals[6], totals[7], totals[8], totals[9])
```

```python
import math
from functools import partial

import jax
import jax.numpy as jnp
from jax import lax
from jax.experimental import pallas as pl
from jax.experimental.pallas import tpu as pltpu
from jax.sharding import Mesh
from jax.sharding import PartitionSpec as P

H = 24
HD = 64
FF = 6144
EPSILON = 1e-05
NEGATIVE = -1e30
SCALE = HD ** (-0.5)
LANES = 2 * HD
CROSS_PAIRS = 4
SEQ = 4
SWAP = [(0, 1), (1, 0)]
BF = jnp.bfloat16
F32 = jnp.float32


def matmul(a, b):
    return jnp.dot(a, b, preferred_element_type=F32)


def contract(a, b, da, db):
    return lax.dot_general(a, b, (((da,), (db,)), ((), ())), preferred_element_type=F32)


def matmul_left(a, b):
    return contract(a, b, 0, 0)


def matmul_right(a, b):
    return contract(a, b, 1, 1)


def norm_forward(values):
    centred = values - jnp.mean(values, axis=-1, keepdims=True)
    inverse = lax.rsqrt(jnp.mean(centred * centred, axis=-1, keepdims=True) + EPSILON)
    return (centred * inverse, inverse)


def norm_backward(grad_normed, normed, inverse):
    inner = jnp.mean(grad_normed * normed, axis=-1, keepdims=True)
    return inverse * (grad_normed - jnp.mean(grad_normed, axis=-1, keepdims=True) - normed * inner)


def gather_dp(part):
    near = lax.all_gather(part, "z", axis=0)
    far = lax.ppermute(near, "x", SWAP)
    low = lax.axis_index("x") == 0
    whole = jnp.stack([jnp.where(low, near, far), jnp.where(low, far, near)], axis=1)
    return whole.reshape(-1, part.shape[-1])


def reduce_dp(partial_sum):
    steps = lax.axis_size("z")
    side = lax.axis_index("x")
    cols = partial_sum.shape[-1]
    split = partial_sum.astype(BF).reshape(steps, 2, -1, cols)
    mine = lax.dynamic_index_in_dim(split, side, 1, keepdims=False)
    other = lax.dynamic_index_in_dim(split, 1 - side, 1, keepdims=False)
    come = lax.ppermute(other, "x", SWAP)
    both = (mine.astype(F32) + come.astype(F32)).astype(BF)
    return lax.psum_scatter(both.reshape(-1, cols), "z", scatter_dimension=0, tiled=True)


def seq_gather(own):
    over = lax.ppermute(own, "y", SWAP)
    core = lax.ppermute(own, "c", SWAP)
    both = lax.ppermute(over, "c", SWAP)
    return [own, core, over, both]


def seq_reduce(parts):
    first = lax.ppermute(parts[1], "c", SWAP)
    second = lax.ppermute(parts[3], "c", SWAP)
    over = (parts[2].astype(F32) + second.astype(F32)).astype(BF)
    come = lax.ppermute(over, "y", SWAP)
    return parts[0].astype(F32) + first.astype(F32) + come.astype(F32)


def seq_exchange(parts):
    core = lax.ppermute(parts[1], "c", SWAP)
    relay = lax.ppermute(parts[3], "c", SWAP)
    over = lax.ppermute(parts[2], "y", SWAP)
    both = lax.ppermute(relay, "y", SWAP)
    return [parts[0], core, over, both]


def in_order(parts):
    odd = lax.axis_index("c") == 1
    up = lax.axis_index("y") == 1
    a, b, c, d = parts
    a, b, c, d = (
        jnp.where(odd, b, a),
        jnp.where(odd, a, b),
        jnp.where(odd, d, c),
        jnp.where(odd, c, d),
    )
    return [jnp.where(up, c, a), jnp.where(up, d, b), jnp.where(up, a, c), jnp.where(up, b, d)]


def turn(value, cosine, sine, back=False):
    lane = lax.broadcasted_iota(jnp.int32, value.shape, 1)
    first = (lane & (HD - 1)) < HD // 2
    swapped = jnp.where(
        first, pltpu.roll(value, LANES - HD // 2, 1), pltpu.roll(value, HD // 2, 1)
    )
    return value * cosine - swapped * sine if back else value * cosine + swapped * sine


def head_lanes(shape, head):
    lane = lax.broadcasted_iota(jnp.int32, shape, 1)
    return (lane >= head * HD) & (lane < (head + 1) * HD)


def self_forward_kernel(q_ref, k_ref, v_ref, cos_ref, sin_ref, bias_ref, o_ref, lse_ref):
    cosine, sine = cos_ref[...], sin_ref[...]
    q = turn(q_ref[...].astype(F32), cosine, sine).astype(BF).astype(F32) * SCALE
    k = turn(k_ref[...].astype(F32), cosine, sine).astype(BF)
    v = v_ref[...]
    outs, stats = [], []
    for head in range(2):
        qh = jnp.where(head_lanes(q.shape, head), q, 0.0).astype(BF)
        scores = contract(qh, k, 1, 1) + bias_ref[0]
        top = jnp.max(scores, axis=1, keepdims=True)
        shifted = jnp.exp(scores - top)
        total = jnp.sum(shifted, axis=1, keepdims=True)
        probs = (shifted * (1.0 / total)).astype(BF)
        outs.append(contract(probs, v, 1, 0))
        stats.append(jnp.broadcast_to(top + jnp.log(total), q.shape))
    low = head_lanes(q.shape, 0)
    o_ref[...] = jnp.where(low, outs[0], outs[1]).astype(BF)
    lse_ref[...] = jnp.where(low, stats[0], stats[1])


def self_backward_kernel(
    q_ref, k_ref, v_ref, d_ref, lse_ref, cos_ref, sin_ref, bias_ref, dq_ref, dk_ref, dv_ref
):
    cosine, sine = cos_ref[...], sin_ref[...]
    q = turn(q_ref[...].astype(F32), cosine, sine).astype(BF).astype(F32) * SCALE
    k = turn(k_ref[...].astype(F32), cosine, sine).astype(BF)
    v = v_ref[...]
    d = d_ref[...]
    full = q.astype(BF)
    dqs, dks, dvs = [], [], []
    for head in range(2):
        inside = head_lanes(q.shape, head)
        qh = jnp.where(inside, q, 0.0).astype(BF)
        dh = jnp.where(inside, d, jnp.zeros_like(d))
        lse = lse_ref[:, head * HD : head * HD + 1]
        probs = jnp.exp(contract(qh, k, 1, 1) + bias_ref[0] - lse)
        grads = contract(dh, v, 1, 1)
        inner = jnp.sum(probs * grads, axis=1, keepdims=True)
        ds = (probs * (grads - inner)).astype(BF)
        dqs.append(contract(ds, k, 1, 0))
        dks.append(contract(ds, full, 0, 0))
        dvs.append(contract(probs.astype(BF), d, 0, 0))
    low = head_lanes(q.shape, 0)
    dq = jnp.where(low, dqs[0], dqs[1]) * SCALE
    dk = jnp.where(low, dks[0], dks[1])
    dq_ref[...] = turn(dq, cosine, sine, back=True).astype(BF)
    dk_ref[...] = turn(dk, cosine, sine, back=True).astype(BF)
    dv_ref[...] = jnp.where(low, dvs[0], dvs[1]).astype(BF)


def self_specs(slots, full, pairs):
    def part(which):
        return pl.BlockSpec((full, LANES), lambda s, h, w=which: (s, w * pairs + h))

    table = pl.BlockSpec((full, LANES), lambda s, h: (0, 0))
    bias = pl.BlockSpec((1, 1, full), lambda s, h: (s, 0, 0))
    block = pl.BlockSpec((full, LANES), lambda s, h: (s, h))
    return part, table, bias, block


def self_forward(qkv, cosine, sine, bias):
    slots, _, full = bias.shape
    pairs = qkv.shape[1] // (3 * LANES)
    part, table, key, block = self_specs(slots, full, pairs)
    shape = (slots * full, pairs * LANES)
    return pl.pallas_call(
        self_forward_kernel,
        grid=(slots, pairs),
        in_specs=[part(0), part(1), part(2), table, table, key],
        out_specs=[block, block],
        out_shape=[jax.ShapeDtypeStruct(shape, BF), jax.ShapeDtypeStruct(shape, F32)],
        name="self_forward",
    )(qkv, qkv, qkv, cosine, sine, bias)


def self_backward(qkv, grad_context, lse, cosine, sine, bias):
    slots, _, full = bias.shape
    pairs = qkv.shape[1] // (3 * LANES)
    part, table, key, block = self_specs(slots, full, pairs)
    shape = jax.ShapeDtypeStruct((slots * full, pairs * LANES), BF)
    return pl.pallas_call(
        self_backward_kernel,
        grid=(slots, pairs),
        in_specs=[part(0), part(1), part(2), block, block, table, table, key],
        out_specs=[block, block, block],
        out_shape=[shape, shape, shape],
        name="self_backward",
    )(qkv, qkv, qkv, grad_context, lse, cosine, sine, bias)


def cross_probs(q, k, count):
    scores = contract(q, k, 1, 1) * SCALE
    token = lax.broadcasted_iota(jnp.int32, scores.shape, 1)
    scores = jnp.where(token < count, scores, NEGATIVE)
    shifted = jnp.exp(scores - jnp.max(scores, axis=1, keepdims=True))
    return shifted * (1.0 / jnp.sum(shifted, axis=1, keepdims=True))


def cross_forward_kernel(count, q_ref, k_ref, v_ref, o_ref):
    for pair in range(q_ref.shape[1] // LANES):
        lanes = slice(pair * LANES, (pair + 1) * LANES)
        q, k, v = q_ref[:, lanes], k_ref[0, :, lanes], v_ref[0, :, lanes]
        outs = []
        for head in range(2):
            qh = jnp.where(head_lanes(q.shape, head), q, jnp.zeros_like(q))
            outs.append(contract(cross_probs(qh, k, count).astype(BF), v, 1, 0))
        o_ref[:, lanes] = jnp.where(head_lanes(q.shape, 0), outs[0], outs[1]).astype(BF)


def cross_backward_kernel(count, q_ref, k_ref, v_ref, d_ref, dq_ref, dk_ref, dv_ref):
    for pair in range(q_ref.shape[1] // LANES):
        lanes = slice(pair * LANES, (pair + 1) * LANES)
        q, k, v, d = q_ref[:, lanes], k_ref[0, :, lanes], v_ref[0, :, lanes], d_ref[:, lanes]
        dqs, dks, dvs = [], [], []
        for head in range(2):
            inside = head_lanes(q.shape, head)
            qh = jnp.where(inside, q, jnp.zeros_like(q))
            dh = jnp.where(inside, d, jnp.zeros_like(d))
            probs = cross_probs(qh, k, count)
            grads = contract(dh, v, 1, 1)
            inner = jnp.sum(probs * grads, axis=1, keepdims=True)
            ds = (probs * (grads - inner)).astype(BF)
            dqs.append(contract(ds, k, 1, 0))
            dks.append(contract(ds, q, 0, 0))
            dvs.append(contract(probs.astype(BF), d, 0, 0))
        low = head_lanes(q.shape, 0)
        far = head_lanes(k.shape, 0)
        dq_ref[:, lanes] = (jnp.where(low, dqs[0], dqs[1]) * SCALE).astype(BF)
        dk_ref[0, :, lanes] = (jnp.where(far, dks[0], dks[1]) * SCALE).astype(BF)
        dv_ref[0, :, lanes] = jnp.where(far, dvs[0], dvs[1]).astype(BF)


def cross_specs(rows, tokens):
    width = CROSS_PAIRS * LANES
    block = pl.BlockSpec((rows, width), lambda s, h: (s, h))
    memory = pl.BlockSpec((1, tokens, width), lambda s, h: (s, 0, h))
    return block, memory


def cross_forward(query, keys, values, count):
    slots, tokens, width = keys.shape
    block, memory = cross_specs(query.shape[0] // slots, tokens)
    return pl.pallas_call(
        partial(cross_forward_kernel, count),
        grid=(slots, width // (CROSS_PAIRS * LANES)),
        in_specs=[block, memory, memory],
        out_specs=block,
        out_shape=jax.ShapeDtypeStruct(query.shape, BF),
        name="cross_forward",
    )(query, keys, values)


def cross_backward(query, keys, values, grad_context, count):
    slots, tokens, width = keys.shape
    block, memory = cross_specs(query.shape[0] // slots, tokens)
    far = jax.ShapeDtypeStruct(keys.shape, BF)
    return pl.pallas_call(
        partial(cross_backward_kernel, count),
        grid=(slots, width // (CROSS_PAIRS * LANES)),
        in_specs=[block, memory, memory, block],
        out_specs=[block, memory, memory],
        out_shape=[jax.ShapeDtypeStruct(query.shape, BF), far, far],
        name="cross_backward",
    )(query, keys, values, grad_context)


def body(
    hidden,
    conditioning,
    slot_sequence,
    lengths,
    self_inputs,
    self_output,
    cross_query,
    cross_memory,
    cross_output,
    feed_expand,
    feed_reduce,
    gain_self,
    gain_cross,
    gain_feed,
    cotangent,
):
    slots, rows, width = hidden.shape
    quarter = width // SEQ
    own = lax.axis_index("y") * 2 + lax.axis_index("c")
    shards = lax.axis_size("z") * 2
    hidden_part = FF // (shards * SEQ)
    full = rows * SEQ
    tokens = slots * full
    local = slots * rows

    def column_quarter(weight):
        pieces = [
            lax.dynamic_slice_in_dim(weight, base + own * quarter, quarter, axis=1)
            for base in range(0, weight.shape[1], width)
        ]
        return jnp.concatenate(pieces, axis=1)

    def scaled(weight, gain):
        return (weight.astype(F32) * gain.astype(F32)[:, None]).astype(BF)

    def gather_whole(weight):
        share = weight.shape[0] // SEQ
        piece = gather_dp(lax.dynamic_slice_in_dim(weight, own * share, share, axis=0))
        pieces = [p.reshape(shards, share, width) for p in seq_gather(piece)]
        return jnp.stack(in_order(pieces), axis=1).reshape(-1, width)

    def reduce_whole(partial_sum):
        share = partial_sum.shape[0] // (shards * SEQ)
        split = partial_sum.astype(BF).reshape(shards, SEQ, share, width)
        parts = [
            lax.dynamic_index_in_dim(split, own ^ r, 1, keepdims=False).reshape(-1, width)
            for r in range(SEQ)
        ]
        return reduce_dp(seq_reduce(parts).astype(BF))

    def spread(value):
        parts = seq_gather(value.reshape(slots, rows, value.shape[-1]))
        return jnp.stack(parts, axis=1).reshape(tokens, value.shape[-1])

    def collect(value):
        split = value.astype(BF).reshape(slots, SEQ, rows, width)
        return seq_reduce([split[:, r] for r in range(SEQ)]).reshape(local, width)

    table = jnp.arange(lengths.shape[0], dtype=jnp.int32)
    length = jnp.sum(jnp.where(table[None, :] == slot_sequence[:, None], lengths[None, :], 0), axis=1)
    row = jnp.arange(rows, dtype=jnp.int32)
    position = jnp.concatenate([(own ^ r) * rows + row for r in range(SEQ)])
    usable = position[None, :] < jnp.maximum(length, 1)[:, None]
    bias = jnp.where(usable, 0.0, NEGATIVE).astype(F32)[:, None, :]
    valid = ((own * rows + row)[None, :] < length[:, None]).astype(F32).reshape(local, 1)
    freqs = jnp.exp(jnp.arange(HD // 2, dtype=F32) * (-2.0 * math.log(10000.0) / HD))
    angles = position.astype(F32)[:, None] * freqs[None, :]
    cos_part, sin_part = jnp.cos(angles), jnp.sin(angles)
    cosine = jnp.concatenate([cos_part] * 4, axis=1)
    sine = jnp.concatenate([-sin_part, sin_part] * 2, axis=1)
    count = conditioning.shape[1]
    index = jnp.minimum(slot_sequence, conditioning.shape[0] - 1)
    memory = jnp.stack(
        [
            lax.dynamic_index_in_dim(conditioning, index[s], 0, keepdims=False)
            for s in range(slots)
        ]
    )
    memory = jnp.pad(memory, ((0, 0), (0, -count % 16), (0, 0)))
    padded = memory.shape[1]
    memory = memory.reshape(slots * padded, -1)

    inputs_w = gather_dp(scaled(column_quarter(self_inputs), gain_self))
    output_w = gather_whole(self_output)
    memory_w = gather_dp(column_quarter(cross_memory))
    query_w = gather_whole(scaled(cross_query, gain_cross))
    cross_w = gather_whole(cross_output)
    split = feed_expand.reshape(-1, 2 * shards, SEQ, hidden_part)
    expand_own = lax.dynamic_index_in_dim(split, own, 2, keepdims=False)
    expand_w = gather_dp(scaled(expand_own.reshape(feed_expand.shape[0], -1), gain_feed))
    reduce_w = gather_dp(
        lax.dynamic_slice_in_dim(feed_reduce, own * hidden_part, hidden_part, axis=0)
    )

    start = hidden.reshape(local, width).astype(F32)
    normed_one, inverse_one = norm_forward(start)
    layer_one = spread(normed_one.astype(BF))
    qkv = matmul(layer_one, inputs_w).astype(BF)
    attended, lse = self_forward(qkv, cosine, sine, bias)
    split = attended.reshape(slots, SEQ, rows, quarter)
    parts = seq_exchange([split[:, r] for r in range(SEQ)])
    context = jnp.concatenate([p.reshape(local, quarter) for p in in_order(parts)], axis=1)
    after_self = start + matmul(context, output_w)

    memory_kv = seq_gather(matmul(memory, memory_w).astype(BF).reshape(slots, padded, -1))
    memory_kv = in_order(memory_kv)
    memory_keys = jnp.concatenate([p[..., :quarter] for p in memory_kv], axis=2)
    memory_vals = jnp.concatenate([p[..., quarter:] for p in memory_kv], axis=2)
    normed_two, inverse_two = norm_forward(after_self)
    layer_two = normed_two.astype(BF)
    cross_q = matmul(layer_two, query_w).astype(BF)
    cross_ctx = cross_forward(cross_q, memory_keys, memory_vals, count)
    after_cross = after_self + matmul(cross_ctx, cross_w)

    normed_three, inverse_three = norm_forward(after_cross)
    layer_three = spread(normed_three.astype(BF))
    expanded = matmul(layer_three, expand_w).astype(BF)
    hidden_units = expanded.shape[1] // 2
    gate = expanded[:, :hidden_units].astype(F32)
    up = expanded[:, hidden_units:].astype(F32)
    sigmoid = 1.0 / (1.0 + jnp.exp(-gate))
    activated = (gate * sigmoid * up).astype(BF)
    result = (after_cross + collect(matmul(activated, reduce_w))) * valid

    grad_three = cotangent.reshape(local, width).astype(F32) * valid
    grad_low = spread(grad_three.astype(BF))
    grad_act = matmul_right(grad_low, reduce_w)
    grad_gate = grad_act * up * sigmoid * (1.0 + gate * (1.0 - sigmoid))
    grad_up = grad_act * gate * sigmoid
    grad_expanded = jnp.concatenate([grad_gate.astype(BF), grad_up.astype(BF)], axis=1)
    sum_reduce = reduce_dp(matmul_left(activated, grad_low))
    sum_expand = reduce_dp(matmul_left(layer_three, grad_expanded))
    grad_normed = collect(matmul_right(grad_expanded, expand_w))
    grad_two = grad_three + norm_backward(grad_normed, normed_three, inverse_three)

    grad_two_low = grad_two.astype(BF)
    sum_cross = reduce_whole(matmul_left(cross_ctx, grad_two_low))
    grad_cctx = matmul_right(grad_two_low, cross_w).astype(BF)
    grad_cq, grad_keys, grad_vals = cross_backward(
        cross_q, memory_keys, memory_vals, grad_cctx, count
    )
    sum_query = reduce_whole(matmul_left(layer_two, grad_cq))
    parts = in_order(
        [
            jnp.concatenate(
                [
                    grad_keys[..., g * quarter : (g + 1) * quarter],
                    grad_vals[..., g * quarter : (g + 1) * quarter],
                ],
                axis=2,
            )
            for g in range(SEQ)
        ]
    )
    grad_memory = seq_reduce(parts).astype(BF).reshape(slots * padded, -1)
    sum_memory = reduce_dp(matmul_left(memory, grad_memory))
    grad_normed = matmul_right(grad_cq, query_w)
    grad_one = grad_two + norm_backward(grad_normed, normed_two, inverse_two)

    grad_one_low = grad_one.astype(BF)
    sum_output = reduce_whole(matmul_left(context, grad_one_low))
    grad_context = matmul_right(grad_one_low, output_w).astype(BF)
    parts = in_order(
        [
            grad_context[:, g * quarter : (g + 1) * quarter].reshape(slots, rows, quarter)
            for g in range(SEQ)
        ]
    )
    grad_heads = jnp.stack(seq_exchange(parts), axis=1).reshape(tokens, quarter)
    grad_qkv = jnp.concatenate(
        self_backward(qkv, grad_heads, lse, cosine, sine, bias), axis=1
    )
    sum_inputs = reduce_dp(matmul_left(layer_one, grad_qkv))
    grad_normed = collect(matmul_right(grad_qkv, inputs_w))
    grad_start = grad_one + norm_backward(grad_normed, normed_one, inverse_one)

    def rows_of(value):
        parts = in_order(seq_gather(value))
        return jnp.concatenate([p.astype(F32) for p in parts], axis=0)

    def columns_of(value, block):
        parts = in_order(seq_gather(value))
        parts = [p.reshape(value.shape[0], -1, block) for p in parts]
        return jnp.stack(parts, axis=2).reshape(value.shape[0], -1).astype(F32)

    def with_gain(total, weight, gain):
        return total * gain.astype(F32)[:, None], jnp.sum(total * weight.astype(F32), axis=1)

    grad_reduce = rows_of(sum_reduce)
    grad_expand, grad_gain_feed = with_gain(columns_of(sum_expand, hidden_part), feed_expand, gain_feed)
    grad_cross = rows_of(sum_cross)
    grad_query, grad_gain_cross = with_gain(rows_of(sum_query), cross_query, gain_cross)
    grad_cmem = columns_of(sum_memory, quarter)
    grad_output = rows_of(sum_output)
    grad_inputs, grad_gain_self = with_gain(columns_of(sum_inputs, quarter), self_inputs, gain_self)
    return (
        result.astype(BF).reshape(hidden.shape),
        grad_start.reshape(hidden.shape),
        grad_inputs,
        grad_output,
        grad_query,
        grad_cmem,
        grad_cross,
        grad_expand,
        grad_reduce,
        grad_gain_self,
        grad_gain_cross,
        grad_gain_feed,
    )


def solution(mesh):
    shards = mesh.shape["dp"]
    grid = Mesh(mesh.devices.reshape(shards // 2, 2, 2, 2), ("z", "x", "y", "c"))
    dp, seq = ("z", "x"), ("y", "c")
    token = P(dp, seq, None)
    weight = P(dp, None)
    gain = P(dp)
    return jax.shard_map(
        body,
        mesh=grid,
        in_specs=(token, P(), P(dp), P()) + (weight,) * 7 + (gain,) * 3 + (token,),
        out_specs=(token, token) + (weight,) * 7 + (gain,) * 3,
        check_vma=False,
    )
```
